256 devices in a mesh: ctx: 128 (over x, y, z), head: 2 (over core).
Axes of the slice: x: 4, y: 4, z: 8, core: 2. Of those that a mesh axis runs over, the one named last changes fastest.
Arguments:
- hidden: bfloat16 [16384, 2048], P(('ctx', 'head')), may hold values from -6 to 6
- w_query: bfloat16 [2048, 2048], P(None, 'head'), may hold values from -0.125 to 0.125
- w_key: bfloat16 [2048, 256], P(None, 'head'), may hold values from -0.125 to 0.125
- w_value: bfloat16 [2048, 256], P(None, 'head'), may hold values from -0.125 to 0.125
- w_dir: bfloat16 [2048, 256], P(None, 'head'), may hold values from -0.125 to 0.125
- u_rate: bfloat16 [2, 2048], P('head'), may hold values from -0.125 to 0.125
- rate_bias: float32 [2], P('head'), may hold values from 5 to 7
- q_gain: float32 [128], replicated, may hold values from 0.8 to 12
- k_gain: float32 [128], replicated, may hold values from 0.8 to 12
- w_out: bfloat16 [2048, 2048], P('head'), may hold values from -0.1875 to 0.1875
- block_mask: int32 [128, 128], P('ctx'), may hold values from 0 to 1, as said below
Outputs:
- layer_out: bfloat16 [16384, 2048], P(('ctx', 'head'))
The draws below stay inside these ranges and needn't reach their ends.
Inputs may be any that keep to these rules, and one draw needn't show every extreme that they name: block_mask[I, J] is 1 only where J < I; each row holds at most 32 ones, and row 127 holds exactly 32.
All inputs are finite; a program needn't handle non-finite values.
Results may differ from the reference program's by a relative error of at most 0.01045.
Values may be sent and summed in bfloat16 or wider, within the bound.
A program may use at most 128 MiB of HBM per device.

```python
import math
import jax
import jax.numpy as jnp
from jax import lax

D = 2048
HD = 128
KVH = 2
GROUP = 8
SEG = 128
QH = 16
NB = 128
TOKENS = 16384
MOSTB = 32


def channel_gains(key, stream):
    uniform_base = jax.random.uniform(jax.random.fold_in(key, stream), (HD,), jnp.float32)
    gain_values = 0.8 * jnp.exp(uniform_base * jnp.log(3.0 / 0.8))
    return gain_values


def draw_q_gain(key, part):
    return channel_gains(key, 5)


def draw_k_gain(key, part):
    return channel_gains(key, 9)


def draw_block_mask(key, part):
    first_key, second_key = jax.random.split(jax.random.fold_in(key, 31))
    third_key = jax.random.fold_in(key, 47)
    rows_index = jnp.arange(NB, dtype=jnp.int32)
    halvings = jax.random.randint(first_key, (NB,), 0, 6, dtype=jnp.int32)
    wanted = jnp.maximum(jnp.right_shift(jnp.full((NB,), MOSTB, jnp.int32), halvings), 1)
    wanted = jnp.where(rows_index == NB - 1, MOSTB, wanted)
    counts = jnp.minimum(wanted, rows_index)
    earlier = rows_index[None, :] < rows_index[:, None]
    scores = jax.random.randint(second_key, (NB, NB), 0, 1 << 20, dtype=jnp.int32) * NB + rows_index[None, :]
    favoured = jax.random.randint(third_key, (NB,), 0, 2, dtype=jnp.int32)
    far_column = rows_index - NB // 2
    pick_far = (rows_index[None, :] == far_column[:, None]) & (favoured[:, None] == 1) & (far_column[:, None] >= 0)
    scores = jnp.where(pick_far, jnp.int32(-1), scores)
    scores = jnp.where(earlier, scores, jnp.int32(1 << 30))
    rank_of = jnp.argsort(jnp.argsort(scores, axis=1, stable=True), axis=1, stable=True)
    return (earlier & (rank_of < counts[:, None])).astype(jnp.int32)


def shard_levels(rng, shape, cuts, least, high):
    loudness, own = 1.0, jax.random.fold_in(rng, 6)
    for position, shards_of in cuts:
        draws = jnp.exp(jax.random.uniform(jax.random.fold_in(own, position), (shards_of,), jnp.float32, least / len(cuts), high / len(cuts)))
        loudness = loudness * jnp.repeat(draws, shape[position] // shards_of).reshape([-1 if axis == position else 1 for axis in range(len(shape))])
    return loudness


def gaussian(own_key, dims, spread, most, cuts=(), held_as=jnp.bfloat16):
    level = shard_levels(own_key, dims, cuts, -0.22, 0.18) if cuts else 1.0
    drawn = jax.random.normal(own_key, dims, jnp.float32) * spread * level
    return jnp.minimum(jnp.maximum(drawn, -most), most).astype(held_as)


def setup_inputs(seed: int = 0) -> dict:
    seeds = jax.random.split(jax.random.key(seed), 12)
    hidden = gaussian(seeds[0], (TOKENS, D), 1.0, 6.0, ((0, 256),))
    w_query = gaussian(seeds[1], (D, QH * HD), D ** -0.5, 0.125, ((1, 2),))
    w_key = gaussian(seeds[2], (D, KVH * HD), D ** -0.5, 0.125, ((1, 2),))
    w_value = gaussian(seeds[3], (D, KVH * HD), D ** -0.5, 0.125, ((1, 2),))
    w_dir = gaussian(seeds[4], (D, KVH * HD), D ** -0.5, 0.125, ((1, 2),))
    u_rate = gaussian(seeds[5], (KVH, D), D ** -0.5, 0.125, ((0, 2),))
    rate_bias = jnp.clip(5.0 + 2.0 * jax.random.uniform(seeds[6], (KVH,), jnp.float32) ** shard_levels(seeds[6], (KVH,), ((0, 2),), -0.2, 0.2), 5.0, 7.0)
    q_gain = draw_q_gain(jax.random.fold_in(seeds[11], 71), 0)
    k_gain = draw_k_gain(jax.random.fold_in(seeds[11], 71), 0)
    w_out = gaussian(seeds[9], (QH * HD, D), (QH * HD // 2) ** -0.5, 0.1875, ((0, 2),))
    block_mask = draw_block_mask(jax.random.fold_in(seeds[11], 71), 0)
    return {"hidden": hidden, "w_query": w_query, "w_key": w_key, "w_value": w_value, "w_dir": w_dir, "u_rate": u_rate, "rate_bias": rate_bias, "q_gain": q_gain, "k_gain": k_gain, "w_out": w_out, "block_mask": block_mask}


HIGHEST = lax.Precision.HIGHEST
EPSILON = 1e-06
NEGATIVE = -1e+30

def rms_scaled(values_in, gain):
    return values_in * lax.rsqrt(lax.optimization_barrier(jnp.mean(values_in * values_in, axis=-1, keepdims=True)) + EPSILON) * gain

def segment_terms(seg_rows, query_cols, key_cols, value_cols, dir_cols, rate_vector, rate_offset, q_gain, k_gain):
    tokens_here = seg_rows.shape[0]
    head_size = key_cols.shape[1]
    groups = query_cols.shape[1] // head_size
    scaling = 1.0 / math.sqrt(head_size)
    queries = jnp.dot(seg_rows.astype(jnp.float32), query_cols.astype(jnp.float32), preferred_element_type=jnp.float32)
    queries = queries.reshape(tokens_here, groups, head_size).transpose(1, 0, 2).reshape(groups * tokens_here, head_size)
    queries = rms_scaled(queries, q_gain)
    key_rows = rms_scaled(jnp.dot(seg_rows.astype(jnp.float32), key_cols.astype(jnp.float32), preferred_element_type=jnp.float32), k_gain)
    value_rows = jnp.dot(seg_rows.astype(jnp.float32), value_cols.astype(jnp.float32), preferred_element_type=jnp.float32).astype(jnp.bfloat16)
    raw_dirs = jnp.dot(seg_rows.astype(jnp.float32), dir_cols.astype(jnp.float32), preferred_element_type=jnp.float32)
    directions = raw_dirs * lax.rsqrt(lax.optimization_barrier(jnp.sum(raw_dirs * raw_dirs, axis=-1, keepdims=True)) + EPSILON)
    rate_values = 2.0 * jax.nn.sigmoid(jnp.dot(seg_rows.astype(jnp.float32), rate_vector.astype(jnp.float32), preferred_element_type=jnp.float32) + rate_offset)
    positions = jnp.arange(tokens_here, dtype=jnp.int32)
    strictly_below = positions[:, None] > positions[None, :]
    up_to = jnp.tile(positions[:, None] >= positions[None, :], (groups, 1))
    gram_matrix = jnp.dot(directions, directions.T, precision=HIGHEST)
    lower_unit = jnp.eye(tokens_here, dtype=directions.dtype) + jnp.where(strictly_below, rate_values[:, None] * gram_matrix, 0.0)
    solved = lax.linalg.triangular_solve(lower_unit, rate_values[:, None] * directions, left_side=True, lower=True, unit_diagonal=True)
    crossing = jnp.where(strictly_below, jnp.dot(directions, key_rows.T, precision=HIGHEST), 0.0)
    coefficients = lax.linalg.triangular_solve(lower_unit, rate_values[:, None] * crossing, left_side=True, lower=True, unit_diagonal=True)
    exit_keys = key_rows - jnp.dot(coefficients.T, directions, precision=HIGHEST)
    product = jnp.eye(head_size, dtype=directions.dtype) - jnp.dot(directions.T, solved, precision=HIGHEST)
    reach_terms = jnp.where(up_to, jnp.dot(queries, directions.T, precision=HIGHEST), 0.0)
    moved_queries = (queries - jnp.dot(reach_terms, solved, precision=HIGHEST)).astype(jnp.bfloat16)
    own_scores = (jnp.dot(queries, key_rows.T, precision=HIGHEST) - jnp.dot(reach_terms, coefficients, precision=HIGHEST)) * scaling
    own_scores = jnp.where(up_to, own_scores, NEGATIVE)
    return (moved_queries, own_scores, exit_keys, value_rows, product)

def reference(hidden, w_query, w_key, w_value, w_dir, u_rate, rate_bias, q_gain, k_gain, w_out, block_mask):
    segments = NB
    scaling = 1.0 / math.sqrt(HD)
    blocks_index = jnp.arange(segments, dtype=jnp.int32)
    head_outputs = []
    for kv_head in range(KVH):
        query_cols = w_query[:, kv_head * GROUP * HD:(kv_head + 1) * GROUP * HD]
        key_cols = w_key[:, kv_head * HD:(kv_head + 1) * HD]
        value_cols = w_value[:, kv_head * HD:(kv_head + 1) * HD]
        dir_cols = w_dir[:, kv_head * HD:(kv_head + 1) * HD]
        rate_vector = u_rate[kv_head]
        rate_offset = rate_bias[kv_head]

        def per_segment(seg_rows):
            return segment_terms(seg_rows, query_cols, key_cols, value_cols, dir_cols, rate_vector, rate_offset, q_gain, k_gain)
        moved_queries, own_scores, exit_keys, value_rows, products = lax.map(per_segment, hidden.reshape(segments, SEG, D))

        def advance(buffer, seg_index):
            allowed = (block_mask[seg_index] > 0) & (blocks_index < seg_index)
            ranking = jnp.where(allowed, 0, 1) * segments + blocks_index
            chosen = jnp.argsort(ranking)[:MOSTB]
            usable = jnp.repeat(allowed[chosen], SEG)
            key_sel = buffer.reshape(segments, SEG, HD)[chosen].reshape(MOSTB * SEG, HD).astype(jnp.bfloat16)
            value_sel = value_rows[chosen].reshape(MOSTB * SEG, HD)
            scores = jnp.dot(moved_queries[seg_index].astype(jnp.float32), key_sel.T.astype(jnp.float32), preferred_element_type=jnp.float32) * scaling
            scores = jnp.where(usable[None, :], scores, NEGATIVE)
            local_scores = own_scores[seg_index]
            peak_score = jnp.maximum(lax.optimization_barrier(jnp.max(scores, axis=1)), lax.optimization_barrier(jnp.max(local_scores, axis=1)))
            far_exp = jnp.exp(scores - peak_score[:, None])
            near_exp = jnp.exp(local_scores - peak_score[:, None])
            total_weight = lax.optimization_barrier(jnp.sum(far_exp, axis=1)) + lax.optimization_barrier(jnp.sum(near_exp, axis=1))
            weighted = jnp.dot(far_exp.astype(jnp.bfloat16).astype(jnp.float32), value_sel.astype(jnp.float32), preferred_element_type=jnp.float32)
            weighted = weighted + jnp.dot(near_exp.astype(jnp.bfloat16).astype(jnp.float32), value_rows[seg_index].astype(jnp.float32), preferred_element_type=jnp.float32)
            attended = (weighted / total_weight[:, None]).astype(jnp.bfloat16)
            buffer = jnp.dot(buffer, products[seg_index].T, precision=HIGHEST)
            buffer = lax.dynamic_update_slice(buffer, exit_keys[seg_index], ((seg_index * SEG).astype(jnp.int32), jnp.int32(0)))
            return (buffer, attended)
        start_buffer = jnp.zeros((segments * SEG, HD), jnp.float32)
        _, attended_all = lax.scan(advance, start_buffer, blocks_index)
        attended_all = attended_all.reshape(segments, GROUP, SEG, HD).transpose(0, 2, 1, 3).reshape(segments * SEG, GROUP * HD)
        head_outputs.append(attended_all)
    joined = jnp.concatenate(head_outputs, axis=1)
    return jnp.dot(joined.astype(jnp.float32), w_out.astype(jnp.float32), preferred_element_type=jnp.float32).astype(jnp.bfloat16)
```

```python
import math

import jax
import jax.numpy as jnp
from jax import lax
from jax.experimental import pallas as pl
from jax.experimental.pallas import tpu as pltpu
from jax.sharding import PartitionSpec as P

HD = 128
SEG = 128
GROUP = 8
MOST = 32
SIZES = (4, 4, 8)
NX, NY, NZ = SIZES
NG = NX * NY
SLICE = SEG // NZ
BLOCK = SEG + SLICE
ROWS = BLOCK // 3
ORDERS = ((2, 1, 0), (0, 2, 1), (1, 0, 2))
EPSILON = 1e-06
NEGATIVE = -1e30
SCALE2 = math.log2(math.e) / math.sqrt(HD)
MESH = pl.DeviceIdType.MESH
F32, BF16 = jnp.float32, jnp.bfloat16
VMEM = pl.BlockSpec(memory_space=pltpu.VMEM)
SMEM = pl.BlockSpec(memory_space=pltpu.SMEM)
ANY = pl.BlockSpec(memory_space=pl.ANY)

NN = ((1,), (0,))
NT = ((1,), (1,))


def mm(a, b, dims=NN):
    return lax.dot_general(a, b, (dims, ((), ())), preferred_element_type=F32)


def split(x):
    hi = x.astype(BF16)
    return hi, (x - hi.astype(F32)).astype(BF16)


def dot3(a, b, dims=NN):
    ah, al = a if isinstance(a, tuple) else split(a)
    bh, bl = b if isinstance(b, tuple) else split(b)
    return mm(ah, bh, dims) + (mm(ah, bl, dims) + mm(al, bh, dims))


def coords():
    c = lax.axis_index("ctx")
    return c // (NY * NZ), (c // NZ) % NY, c % NZ


def neighbour(me, axis, delta):
    t = list(me)
    t[axis] = (me[axis] + delta) % SIZES[axis]
    return (t[0] * NY + t[1]) * NZ + t[2]


def swap_kernel(src, dst, send_sem, recv_sem):
    other = 1 - lax.axis_index("head")
    barrier = pltpu.get_barrier_semaphore()
    pl.semaphore_signal(barrier, inc=1, device_id={"head": other}, device_id_type=MESH)
    pl.semaphore_wait(barrier, 1)
    copy = pltpu.make_async_remote_copy(
        src, dst, send_sem, recv_sem, device_id={"head": other}, device_id_type=MESH
    )
    copy.start()
    copy.wait()


def swap(x, collective_id):
    return pl.pallas_call(
        swap_kernel,
        name="swap%d" % collective_id,
        out_shape=jax.ShapeDtypeStruct(x.shape, x.dtype),
        in_specs=[VMEM],
        out_specs=VMEM,
        scratch_shapes=[pltpu.SemaphoreType.DMA, pltpu.SemaphoreType.DMA],
        compiler_params=pltpu.CompilerParams(collective_id=collective_id, has_side_effects=True),
    )(x)


def segment_kernel(
    mine, theirs, wq_hbm, wk, wv, wd, ur, rb, qg, kg,
    mq_o, own_o, pay_o, exit_o, val_o, wq, rows, sem,
):
    load = pltpu.make_async_copy(wq_hbm, wq, sem)
    load.start()
    head = lax.axis_index("head")
    half = SEG // 2
    rows[pl.ds(pl.multiple_of(head * half, half), half), :] = mine[...]
    rows[pl.ds(pl.multiple_of((1 - head) * half, half), half), :] = theirs[...]
    x = rows[...]
    ii = lax.broadcasted_iota(jnp.int32, (SEG, SEG), 0)
    jj = lax.broadcasted_iota(jnp.int32, (SEG, SEG), 1)
    strict = ii > jj
    eye = jnp.where(ii == jj, 1.0, 0.0).astype(F32)

    raw = mm(x, wd[...])
    dirs = raw * lax.rsqrt(jnp.sum(raw * raw, axis=1, keepdims=True) + EPSILON)
    key = mm(x, wk[...])
    key = key * lax.rsqrt(jnp.mean(key * key, axis=1, keepdims=True) + EPSILON) * kg[...]
    logit = jnp.sum(x.astype(F32) * ur[...].astype(F32), axis=1, keepdims=True) + rb[0]
    rate = 2.0 * jax.nn.sigmoid(logit)
    val_o[...] = mm(x, wv[...]).astype(BF16)

    both = jnp.concatenate([dirs, key], axis=0)
    both_s = split(both)
    dirs_s = (both_s[0][:SEG], both_s[1][:SEG])
    grams = dot3(dirs_s, both_s, NT)
    lower = jnp.where(strict, rate * grams[:, :SEG], 0.0)
    crossing = jnp.where(strict, grams[:, SEG:], 0.0)
    size = 1
    inverse = None
    while size < SEG:
        pick = (ii // (2 * size) == jj // (2 * size)) & (ii // size > jj // size)
        corner = jnp.where(pick, lower, 0.0)
        if inverse is None:
            inverse = eye - corner
        else:
            inv_s = split(inverse)
            inverse = inverse - dot3(dot3(inv_s, corner), inv_s)
        size *= 2
    solved = dot3(inverse, jnp.concatenate([rate * dirs, rate * crossing], axis=1))
    solved_s = split(solved)
    turned = dot3(split(solved.T), dirs_s)
    product_t = eye - turned[:SEG]
    exit_keys = key - turned[SEG:]
    hi, lo = split(product_t)
    pay_o[:, 0:HD] = hi
    pay_o[:, HD : 2 * HD] = lo
    pay_o[:, 2 * HD : 3 * HD] = exit_keys.astype(BF16)
    exit_o[...] = exit_keys

    load.wait()
    reach_mask = ii >= jj
    for pair in range(GROUP // 2):
        q2 = mm(x, wq[:, pair * 2 * HD : (pair + 1) * 2 * HD])
        for sub in range(2):
            g = pair * 2 + sub
            q = q2[:, sub * HD : (sub + 1) * HD]
            q = q * lax.rsqrt(jnp.mean(q * q, axis=1, keepdims=True) + EPSILON) * qg[...]
            r = dot3(q, both_s, NT)
            reach = jnp.where(reach_mask, r[:, :SEG], 0.0)
            moved = dot3(reach, solved_s)
            mq_o[g * SEG : (g + 1) * SEG, :] = (q - moved[:, :HD]).astype(BF16)
            own = (r[:, SEG:] - moved[:, HD:]) * SCALE2
            own_o[g * SEG : (g + 1) * SEG, :] = jnp.where(reach_mask, own, NEGATIVE)


def segment(mine, theirs, w_query, w_key, w_value, w_dir, u_rate, rate_bias, q_gain, k_gain):
    sd = jax.ShapeDtypeStruct
    return pl.pallas_call(
        segment_kernel,
        name="segment",
        out_shape=(
            sd((GROUP * SEG, HD), BF16),
            sd((GROUP * SEG, SEG), F32),
            sd((SEG, 3 * HD), BF16),
            sd((SEG, HD), F32),
            sd((SEG, HD), BF16),
        ),
        in_specs=[VMEM, VMEM, ANY, VMEM, VMEM, VMEM, VMEM, SMEM, VMEM, VMEM],
        out_specs=(VMEM,) * 5,
        scratch_shapes=[
            pltpu.VMEM(w_query.shape, BF16),
            pltpu.VMEM((SEG, w_query.shape[0]), BF16),
            pltpu.SemaphoreType.DMA,
        ],
    )(mine, theirs, w_query, w_key, w_value, w_dir, u_rate, rate_bias,
      q_gain.reshape(1, HD), k_gain.reshape(1, HD))


def ring_kernel(pay, out, send_sem, recv_sem, own_sem):
    me = coords()
    z = me[2]
    ahead, behind = neighbour(me, 2, 1), neighbour(me, 2, -1)
    barrier = pltpu.get_barrier_semaphore()
    for other in (ahead, behind):
        pl.semaphore_signal(barrier, inc=1, device_id={"ctx": other}, device_id_type=MESH)
    own = pltpu.make_async_copy(pay, out.at[z], own_sem)
    own.start()
    pl.semaphore_wait(barrier, 2)
    sends, arrived = [], ()
    half = SEG // 2
    for step in range(1, NZ // 2 + 1):
        for c in arrived:
            c.wait_recv()
        new = []
        for di, d in enumerate((1, -1)):
            pos = (z - d * (step - 1)) % NZ
            part = pl.ds(di * half, half) if step == NZ // 2 else pl.ds(0, SEG)
            src = pay if step == 1 else out.at[pos, part]
            c = pltpu.make_async_remote_copy(
                src, out.at[pos, part], send_sem.at[step - 1, di], recv_sem.at[step - 1, di],
                device_id={"ctx": ahead if d == 1 else behind}, device_id_type=MESH,
            )
            c.start()
            new.append(c)
        sends += new
        arrived = new
    for c in arrived:
        c.wait_recv()
    for c in sends:
        c.wait_send()
    own.wait()


def ring(pay):
    return pl.pallas_call(
        ring_kernel,
        name="ring",
        out_shape=jax.ShapeDtypeStruct((NZ,) + pay.shape, pay.dtype),
        in_specs=[VMEM],
        out_specs=VMEM,
        scratch_shapes=[
            pltpu.SemaphoreType.DMA((NZ // 2, 2)),
            pltpu.SemaphoreType.DMA((NZ // 2, 2)),
            pltpu.SemaphoreType.DMA,
        ],
        compiler_params=pltpu.CompilerParams(collective_id=1, has_side_effects=True),
    )(pay)


def store_pair(ref, index, x):
    hi, lo = split(x)
    ref[index, 0:HD, :] = hi
    ref[index, HD : 2 * HD, :] = lo


def chain_kernel(group, exit_keys, val, blk_o, inner_o, lead_o, reach, whole):
    z = lax.axis_index("ctx") % NZ
    ii = lax.broadcasted_iota(jnp.int32, (HD, HD), 0)
    jj = lax.broadcasted_iota(jnp.int32, (HD, HD), 1)
    eye = jnp.where(ii == jj, 1.0, 0.0).astype(F32)
    after, lead = eye, eye
    reach[...] = eye
    for k in range(NZ - 1, -1, -1):
        step = (group[k, :, 0:HD], group[k, :, HD : 2 * HD])
        if k < NZ - 1:
            @pl.when(z == k)
            def _(after=after):
                reach[...] = after
            store_pair(inner_o, k, lead * SCALE2)
            lead = jnp.where(k < z, dot3(step, lead), lead)
            after = dot3(step, after)
        else:
            after = step[0].astype(F32) + step[1].astype(F32)
    lead_o[...] = lead
    hi, lo = split(after)
    whole[:, 0:HD] = hi
    whole[:, HD : 2 * HD] = lo
    blk_o[0:SEG, 0:HD] = dot3(exit_keys[...], reach[...]).astype(BF16)
    blk_o[0:SEG, HD : 2 * HD] = val[...]
    blk_o[SEG:BLOCK, :] = whole[pl.ds(pl.multiple_of(z * SLICE, SLICE), SLICE), :]


def chains(group, exit_keys, val):
    sd = jax.ShapeDtypeStruct
    return pl.pallas_call(
        chain_kernel,
        name="chains",
        out_shape=(
            sd((BLOCK, 2 * HD), BF16),
            sd((NZ - 1, 2 * HD, HD), BF16),
            sd((HD, HD), F32),
        ),
        in_specs=[VMEM] * 3,
        out_specs=(VMEM,) * 3,
        scratch_shapes=[pltpu.VMEM((HD, HD), F32), pltpu.VMEM((HD, 2 * HD), BF16)],
    )(group, exit_keys, val)


def schedule(latency=1.7, unit=0.53):
    events = []
    for s, order in enumerate(ORDERS):
        t, bundle, k = 0.0, 1, 0
        for axis in order:
            n = SIZES[axis]
            for step in range(1, n // 2 + 1):
                events.append((t, s, k, axis, step))
                t += latency + unit * bundle * (0.5 if step == n // 2 else 1.0)
                k += 1
            bundle *= n
    return sorted(events)


def gather_kernel(blk, out, send_sem, recv_sem, own_sem):
    me = coords()
    barrier = pltpu.get_barrier_semaphore()
    for axis in range(3):
        for d in (1, -1):
            pl.semaphore_signal(
                barrier, inc=1, device_id={"ctx": neighbour(me, axis, d)}, device_id_type=MESH
            )
    own = pltpu.make_async_copy(blk, out.at[me[0], me[1], me[2]], own_sem)
    own.start()
    own.wait()
    pl.semaphore_wait(barrier, 6)

    def view(s, axis, pos, lanes):
        done = ORDERS[s][: ORDERS[s].index(axis)]
        idx = [pos if a == axis else slice(None) if a in done else me[a] for a in range(3)]
        return out.at[idx[0], idx[1], idx[2], pl.ds(s * ROWS, ROWS), lanes]

    pending, sends = {}, []
    for _, s, k, axis, step in schedule():
        n = SIZES[axis]
        for c in pending.pop(s, ()):
            c.wait_recv()
        new = []
        for di, d in enumerate((1, -1)):
            pos = (me[axis] - d * (step - 1)) % n
            lanes = pl.ds(di * HD, HD) if step == n // 2 else slice(None)
            ref = view(s, axis, pos, lanes)
            c = pltpu.make_async_remote_copy(
                ref, ref, send_sem.at[s, k, di], recv_sem.at[s, k, di],
                device_id={"ctx": neighbour(me, axis, d)}, device_id_type=MESH,
            )
            c.start()
            new.append(c)
        sends += new
        pending[s] = new
    for s in range(3):
        for c in pending.pop(s, ()):
            c.wait_recv()
    for c in sends:
        c.wait_send()


def gather(blk):
    steps = sum(n // 2 for n in SIZES)
    return pl.pallas_call(
        gather_kernel,
        name="gather",
        out_shape=jax.ShapeDtypeStruct(SIZES + blk.shape, blk.dtype),
        in_specs=[VMEM],
        out_specs=ANY,
        scratch_shapes=[
            pltpu.SemaphoreType.DMA((3, steps, 2)),
            pltpu.SemaphoreType.DMA((3, steps, 2)),
            pltpu.SemaphoreType.DMA,
        ],
        compiler_params=pltpu.CompilerParams(collective_id=2, has_side_effects=True),
    )(blk)


STEP = 4
TILE = 256


def attend_kernel(
    mask, gathered, group, inner, lead, mq, own, val, wo_hbm,
    mine_o, send_o,
    chosen, kv, slices, moves, run, keys, peak, total, acc, att, wo, part, kv_sem, misc_sem,
):
    position = lax.axis_index("ctx")
    me_group, head = position // NZ, lax.axis_index("head")
    w_load = pltpu.make_async_copy(wo_hbm, wo, misc_sem.at[0])
    g_load = pltpu.make_async_copy(gathered.at[:, :, SEG:BLOCK, :], slices, misc_sem.at[1])
    g_load.start()

    def scan(j, count):
        hit = mask[0, j] > 0

        @pl.when(hit)
        def _():
            chosen[count] = j

        return count + hit.astype(jnp.int32)

    count = jnp.minimum(lax.fori_loop(0, position, scan, jnp.int32(0)), MOST)
    chunks = (count + STEP - 1) // STEP

    def fetch(s, _):
        j = chosen[s]
        g, z = j // NZ, j % NZ

        @pl.when(g == me_group)
        def _():
            for src, lanes in ((group.at[z, :, 2 * HD : 3 * HD], 0), (gathered.at[g, z, 0:SEG, HD : 2 * HD], HD)):
                pltpu.make_async_copy(src, kv.at[s, :, lanes : lanes + HD], kv_sem.at[s]).start()

        @pl.when(g != me_group)
        def _():
            pltpu.make_async_copy(gathered.at[g, z, 0:SEG, :], kv.at[s], kv_sem.at[s]).start()

        return 0

    lax.fori_loop(0, count, fetch, 0)
    w_load.start()

    def blank(s, _):
        kv[s] = jnp.zeros((SEG, 2 * HD), BF16)
        return 0

    lax.fori_loop(count, chunks * STEP, blank, 0)

    v_own = val[...]
    for t in range(GROUP * SEG // TILE):
        sl = pl.ds(t * TILE, TILE)
        s = own[sl, :]
        top = jnp.broadcast_to(jnp.max(s, axis=1, keepdims=True), (TILE, HD))
        p = jnp.exp2(s - top)
        peak[sl, :] = top
        total[sl, :] = p
        acc[sl, :] = mm(p.astype(BF16), v_own)

    g_load.wait()

    run[...] = lead[...]

    def step_back(i, _):
        n = me_group - 1 - i
        r = run[...]
        store_pair(moves, n, r * SCALE2)
        g = slices[n].reshape(HD, 2 * HD)
        run[...] = dot3((g[:, 0:HD], g[:, HD : 2 * HD]), r)
        return 0

    lax.fori_loop(0, me_group, step_back, 0)
    moves[NG : NG + NZ - 1] = inner[...]

    def chunk(c, _):
        for u in range(STEP):
            s = c * STEP + u

            @pl.when(s < count)
            def _():
                pltpu.make_async_copy(gathered.at[0, 0, 0:SEG, :], kv.at[s], kv_sem.at[s]).wait()

        for u in range(STEP):
            s = c * STEP + u
            j = jnp.where(s < count, chosen[s], 0)
            which = jnp.where(j // NZ == me_group, NG + j % NZ, j // NZ)
            k = kv[s, :, 0:HD]
            moved = mm(jnp.concatenate([k, k], axis=1), moves[which])
            keys[u * SEG : (u + 1) * SEG, :] = moved.astype(BF16)

        bias = jnp.concatenate(
            [jnp.full((1, SEG), jnp.where(c * STEP + u < count, 0.0, NEGATIVE), F32) for u in range(STEP)], axis=1
        )
        k_now = keys[...]
        v_now = jnp.concatenate([kv[c * STEP + u, :, HD : 2 * HD] for u in range(STEP)], axis=0)
        for t in range(GROUP * SEG // TILE):
            sl = pl.ds(t * TILE, TILE)
            s = mm(mq[sl, :], k_now, NT) + bias
            parts = [s[:, u * SEG : (u + 1) * SEG] for u in range(STEP)]
            high = parts[0]
            for x in parts[1:]:
                high = jnp.maximum(high, x)
            old = peak[sl, :]
            top = jnp.maximum(old, jnp.max(high, axis=1, keepdims=True))
            fade = jnp.exp2(old - top)
            ps = [jnp.exp2(x - top) for x in parts]
            peak[sl, :] = top
            total[sl, :] = total[sl, :] * fade + ((ps[0] + ps[1]) + (ps[2] + ps[3]))
            p = jnp.concatenate([x.astype(BF16) for x in ps], axis=1)
            acc[sl, :] = acc[sl, :] * fade + mm(p, v_now)
        return 0

    lax.fori_loop(0, chunks, chunk, 0)
    for g in range(GROUP):
        sl = pl.ds(g * SEG, SEG)
        out = acc[sl, :] / jnp.sum(total[sl, :], axis=1, keepdims=True)
        att[:, g * HD : (g + 1) * HD] = out.astype(BF16)
    w_load.wait()
    width = wo.shape[1]
    for c in range(0, width, 512):
        part[:, c : c + 512] = mm(att[...], wo[:, c : c + 512])
    half = SEG // 2
    mine_o[...] = part[pl.ds(pl.multiple_of(head * half, half), half), :]
    send_o[...] = part[pl.ds(pl.multiple_of((1 - head) * half, half), half), :].astype(BF16)


def attend(mask, gathered, group, inner, lead, mq, own, val, w_out):
    sd = jax.ShapeDtypeStruct
    width = w_out.shape[1]
    rows = GROUP * SEG
    return pl.pallas_call(
        attend_kernel,
        name="attend",
        out_shape=(sd((SEG // 2, width), F32), sd((SEG // 2, width), BF16)),
        in_specs=[SMEM, ANY, ANY, VMEM, VMEM, VMEM, VMEM, VMEM, ANY],
        out_specs=(VMEM, VMEM),
        scratch_shapes=[
            pltpu.SMEM((MOST,), jnp.int32),
            pltpu.VMEM((MOST, SEG, 2 * HD), BF16),
            pltpu.VMEM((NG, NZ, SLICE, 2 * HD), BF16),
            pltpu.VMEM((NG + NZ - 1, 2 * HD, HD), BF16),
            pltpu.VMEM((HD, HD), F32),
            pltpu.VMEM((STEP * SEG, HD), BF16),
            pltpu.VMEM((rows, HD), F32),
            pltpu.VMEM((rows, HD), F32),
            pltpu.VMEM((rows, HD), F32),
            pltpu.VMEM((SEG, GROUP * HD), BF16),
            pltpu.VMEM(w_out.shape, BF16),
            pltpu.VMEM((SEG, width), F32),
            pltpu.SemaphoreType.DMA((MOST,)),
            pltpu.SemaphoreType.DMA((2,)),
        ],
    )(mask, gathered.reshape(NG, NZ, BLOCK, 2 * HD), group, inner, lead, mq, own, val, w_out)


def body(
    hidden, w_query, w_key, w_value, w_dir, u_rate, rate_bias, q_gain, k_gain, w_out, block_mask
):
    theirs = swap(hidden, 0)
    mq, own, pay, exit_keys, val = segment(
        hidden, theirs, w_query, w_key, w_value, w_dir, u_rate, rate_bias, q_gain, k_gain
    )
    group = ring(pay)
    blk, inner, lead = chains(group, exit_keys, val)
    gathered = gather(blk)
    mine, give = attend(block_mask, gathered, group, inner, lead, mq, own, val, w_out)
    got = swap(give, 3)
    return (mine + got.astype(F32)).astype(BF16)


def solution(mesh):
    in_specs = (
        P(("ctx", "head"), None),
        P(None, "head"),
        P(None, "head"),
        P(None, "head"),
        P(None, "head"),
        P("head", None),
        P("head"),
        P(),
        P(),
        P("head", None),
        P("ctx", None),
    )
    out_specs = P(("ctx", "head"), None)
    return jax.shard_map(body, mesh=mesh, in_specs=in_specs, out_specs=out_specs, check_vma=False)
```

```python
import functools
import heapq
import math

import jax
import jax.numpy as jnp
from jax import lax
from jax.experimental import pallas as pl
from jax.experimental.pallas import tpu as pltpu
from jax.sharding import PartitionSpec as P

HD = 128
SEG = 128
GROUP = 8
MOST = 32
SIZES = (4, 4, 8)
NX, NY, NZ = SIZES
NG = NX * NY
SLICE = SEG // NZ
BLOCK = SEG + 2 * SLICE
ORDERS = ((2, 1, 0), (0, 2, 1), (1, 0, 2))
EPSILON = 1e-06
NEGATIVE = -1e30
SCALE2 = math.log2(math.e) / math.sqrt(HD)
MESH = pl.DeviceIdType.MESH
F32, BF16 = jnp.float32, jnp.bfloat16
VMEM = pl.BlockSpec(memory_space=pltpu.VMEM)
SMEM = pl.BlockSpec(memory_space=pltpu.SMEM)
ANY = pl.BlockSpec(memory_space=pl.ANY)

NN = ((1,), (0,))
NT = ((1,), (1,))


def mm(a, b, dims=NN):
    return lax.dot_general(a, b, (dims, ((), ())), preferred_element_type=F32)


def split(x):
    hi = x.astype(BF16)
    return hi, (x - hi.astype(F32)).astype(BF16)


def dot3(a, b, dims=NN):
    ah, al = a if isinstance(a, tuple) else split(a)
    bh, bl = b if isinstance(b, tuple) else split(b)
    return mm(ah, bh, dims) + (mm(ah, bl, dims) + mm(al, bh, dims))


def coords():
    c = lax.axis_index("ctx")
    return c // (NY * NZ), (c // NZ) % NY, c % NZ


def neighbour(me, axis, delta):
    t = list(me)
    t[axis] = (me[axis] + delta) % SIZES[axis]
    return (t[0] * NY + t[1]) * NZ + t[2]


def swap_kernel(src, dst, send_sem, recv_sem):
    other = 1 - lax.axis_index("head")
    barrier = pltpu.get_barrier_semaphore()
    pl.semaphore_signal(barrier, inc=1, device_id={"head": other}, device_id_type=MESH)
    pl.semaphore_wait(barrier, 1)
    copy = pltpu.make_async_remote_copy(
        src, dst, send_sem, recv_sem, device_id={"head": other}, device_id_type=MESH
    )
    copy.start()
    copy.wait()


def swap(x, collective_id):
    return pl.pallas_call(
        swap_kernel,
        name="swap%d" % collective_id,
        out_shape=jax.ShapeDtypeStruct(x.shape, x.dtype),
        in_specs=[VMEM],
        out_specs=VMEM,
        scratch_shapes=[pltpu.SemaphoreType.DMA, pltpu.SemaphoreType.DMA],
        compiler_params=pltpu.CompilerParams(collective_id=collective_id, has_side_effects=True),
    )(x)


def segment_kernel(
    mine, theirs, wq_hbm, wk, wv, wd, ur, rb, qg, kg,
    mq_o, own_o, pay_o, exit_o, val_o, wq, rows, sem,
):
    load = pltpu.make_async_copy(wq_hbm, wq, sem)
    load.start()
    head = lax.axis_index("head")
    half = SEG // 2
    rows[pl.ds(pl.multiple_of(head * half, half), half), :] = mine[...]
    rows[pl.ds(pl.multiple_of((1 - head) * half, half), half), :] = theirs[...]
    x = rows[...]
    ii = lax.broadcasted_iota(jnp.int32, (SEG, SEG), 0)
    jj = lax.broadcasted_iota(jnp.int32, (SEG, SEG), 1)
    strict = ii > jj
    eye = jnp.where(ii == jj, 1.0, 0.0).astype(F32)

    raw = mm(x, wd[...])
    dirs = raw * lax.rsqrt(jnp.sum(raw * raw, axis=1, keepdims=True) + EPSILON)
    key = mm(x, wk[...])
    key = key * lax.rsqrt(jnp.mean(key * key, axis=1, keepdims=True) + EPSILON) * kg[...]
    logit = jnp.sum(x.astype(F32) * ur[...].astype(F32), axis=1, keepdims=True) + rb[0]
    rate = 2.0 * jax.nn.sigmoid(logit)
    val_o[...] = mm(x, wv[...]).astype(BF16)

    both = jnp.concatenate([dirs, key], axis=0)
    both_s = split(both)
    dirs_s = (both_s[0][:SEG], both_s[1][:SEG])
    grams = dot3(dirs_s, both_s, NT)
    lower = jnp.where(strict, rate * grams[:, :SEG], 0.0)
    crossing = jnp.where(strict, grams[:, SEG:], 0.0)
    size = 1
    inverse = None
    while size < SEG:
        pick = (ii // (2 * size) == jj // (2 * size)) & (ii // size > jj // size)
        corner = jnp.where(pick, lower, 0.0)
        if inverse is None:
            inverse = eye - corner
        else:
            inv_s = split(inverse)
            inverse = inverse - dot3(dot3(inv_s, corner), inv_s)
        size *= 2
    solved = dot3(inverse, jnp.concatenate([rate * dirs, rate * crossing], axis=1))
    solved_s = split(solved)
    turned = dot3(split(solved.T), dirs_s)
    product_t = eye - turned[:SEG]
    exit_keys = key - turned[SEG:]
    hi, lo = split(product_t)
    pay_o[0:HD, :] = hi
    pay_o[HD : 2 * HD, :] = lo
    pay_o[2 * HD : 3 * HD, :] = exit_keys.astype(BF16)
    exit_o[...] = exit_keys

    load.wait()
    reach_mask = ii >= jj
    for pair in range(GROUP // 2):
        q2 = mm(x, wq[:, pair * 2 * HD : (pair + 1) * 2 * HD])
        for sub in range(2):
            g = pair * 2 + sub
            q = q2[:, sub * HD : (sub + 1) * HD]
            q = q * lax.rsqrt(jnp.mean(q * q, axis=1, keepdims=True) + EPSILON) * qg[...]
            r = dot3(q, both_s, NT)
            reach = jnp.where(reach_mask, r[:, :SEG], 0.0)
            moved = dot3(reach, solved_s)
            mq_o[g * SEG : (g + 1) * SEG, :] = (q - moved[:, :HD]).astype(BF16)
            own = (r[:, SEG:] - moved[:, HD:]) * SCALE2
            own_o[g * SEG : (g + 1) * SEG, :] = jnp.where(reach_mask, own, NEGATIVE)


def segment(mine, theirs, w_query, w_key, w_value, w_dir, u_rate, rate_bias, q_gain, k_gain):
    sd = jax.ShapeDtypeStruct
    return pl.pallas_call(
        segment_kernel,
        name="segment",
        out_shape=(
            sd((GROUP * SEG, HD), BF16),
            sd((GROUP * SEG, SEG), F32),
            sd((3 * HD, SEG), BF16),
            sd((SEG, HD), F32),
            sd((SEG, HD), BF16),
        ),
        in_specs=[VMEM, VMEM, ANY, VMEM, VMEM, VMEM, VMEM, SMEM, VMEM, VMEM],
        out_specs=(VMEM,) * 5,
        scratch_shapes=[
            pltpu.VMEM(w_query.shape, BF16),
            pltpu.VMEM((SEG, w_query.shape[0]), BF16),
            pltpu.SemaphoreType.DMA,
        ],
    )(mine, theirs, w_query, w_key, w_value, w_dir, u_rate, rate_bias,
      q_gain.reshape(1, HD), k_gain.reshape(1, HD))


def store_pair(ref, index, x):
    hi, lo = split(x)
    ref[index, 0:HD, :] = hi
    ref[index, HD : 2 * HD, :] = lo


LATENCY, WIRE = 2.5, 42e3


class Stream:
    def __init__(self, name, order, start, rows):
        self.name, self.order, self.start, self.rows = name, order, start, rows


def plan(streams, late, needs, tasks, fillers):
    link, heap, actions, got = {}, [], [], {}
    clock = 0.0
    fillers, tasks = list(fillers), list(tasks)
    missing = sum(SIZES[streams[s].order[0]] - 1 for s in needs)

    def push(t, event):
        heapq.heappush(heap, (t, len(actions), event))

    def ring(s, phase, sub, pieces):
        for di in (0, 1):
            send(s, phase, sub, 1, di, pieces)

    def send(s, phase, sub, step, di, pieces):
        axis = streams[s].order[phase]
        share = 0.5 if step == SIZES[axis] // 2 else 1.0
        begin = max(link.get((axis, di), 0.0), clock)
        link[axis, di] = begin + streams[s].rows * HD * 2 * pieces * share / WIRE
        push(link[axis, di] + LATENCY, ("wait", s, phase, sub, step, di, pieces))
        actions.append(("send", s, phase, sub, step, di))

    def launch(some):
        for s in some:
            for phase in range(min(2, len(streams[s].order))):
                ring(s, phase, 0, 1)

    launch(s for s in range(len(streams)) if s not in late)
    while heap:
        t, _, event = heapq.heappop(heap)
        while fillers and t - clock > 0.6 * fillers[0][1]:
            actions.append(fillers[0][0])
            clock += fillers.pop(0)[1]
        clock = max(clock, t) + 0.03
        if event[0] == "task":
            name, cost = tasks.pop(0)
            actions.append(name)
            clock += cost
            if tasks:
                push(clock, ("task",))
            else:
                launch(late)
            continue
        _, s, phase, sub, step, di, pieces = event
        actions.append(("wait", s, phase, sub, step, di))
        order = streams[s].order
        n = SIZES[order[phase]]
        last = step == n // 2
        if not last:
            send(s, phase, sub, step + 1, di, pieces)
        offset = step if di or last else -step
        got[s, phase, sub, offset] = got.get((s, phase, sub, offset), 0) + (1 if last else 2)
        if got[s, phase, sub, offset] < 2:
            continue
        if s in needs:
            missing -= 1
            if missing == 0:
                push(clock, ("task",))
        if len(order) == 1 or phase == 2:
            continue
        if phase == 0:
            ring(s, 1, offset, 1)
            done = (s, 0)
        else:
            done = (s, offset)
        got[done] = got.get(done, 0) + 1
        if phase == 0 and got[done] == n - 1:
            ring(s, 2, 0, n)
        elif phase == 1 and got[done] == SIZES[order[0]]:
            ring(s, 2, offset, SIZES[order[0]])
    return actions + [f[0] for f in fillers]


def greet(me, axes):
    barrier = pltpu.get_barrier_semaphore()
    for axis in axes:
        for d in (1, -1):
            pl.semaphore_signal(
                barrier, inc=1, device_id={"ctx": neighbour(me, axis, d)}, device_id_type=MESH
            )
    pl.semaphore_wait(barrier, 2 * len(axes))


def core_kernel(
    streams, actions,
    pay, val, exit_keys,
    group, v_all, k_all, inner_o, lead_o,
    blk, reach, whole, after, lead, send_sem, recv_sem, own_sem,
):
    me = coords()
    z = me[2]
    sources = {"pay": pay, "val": val, "blk": blk}
    outs = {"pay": group, "val": v_all, "blk": k_all}
    own = {
        name: pltpu.make_async_copy(
            sources[name], outs[name].at[(z,) if name == "pay" else tuple(me)], own_sem.at[i]
        )
        for i, name in enumerate(sources)
    }
    own["pay"].start()
    own["val"].start()
    greet(me, range(3))
    landed, copies = set(), {}

    def land(name):
        if name not in landed:
            own[name].wait()
            landed.add(name)

    def chain(k):
        if k == NZ - 1:
            land("pay")
            ii = lax.broadcasted_iota(jnp.int32, (HD, HD), 0)
            jj = lax.broadcasted_iota(jnp.int32, (HD, HD), 1)
            eye = jnp.where(ii == jj, 1.0, 0.0).astype(F32)
            reach[...] = eye
            lead[...] = eye
            after[...] = group[k, 0:HD, :].astype(F32) + group[k, HD : 2 * HD, :].astype(F32)
            return
        step = (group[k, 0:HD, :], group[k, HD : 2 * HD, :])

        @pl.when(z == k)
        def _():
            reach[...] = after[...]

        before = lead[...]
        store_pair(inner_o, k, before * SCALE2)
        lead[...] = jnp.where(k < z, dot3(step, before), before)
        after[...] = dot3(step, after[...])

    def emit():
        lead_o[...] = lead[...]
        hi, lo = split(after[...])
        whole[0] = hi
        whole[1] = lo
        part = pl.ds(pl.multiple_of(z * SLICE, SLICE), SLICE)
        blk[SEG : SEG + SLICE, :] = whole[0, part, :]
        blk[SEG + SLICE : BLOCK, :] = whole[1, part, :]
        blk[0:SEG, :] = dot3(exit_keys[...], reach[...]).astype(BF16)
        own["blk"].start()

    for act in actions:
        if act[0] == "chain":
            chain(act[1])
            continue
        if act[0] == "emit":
            emit()
            continue
        key = act[1:]
        s, phase, sub, step, di = key
        if act[0] == "wait":
            if key in copies:
                copies[key].wait_recv()
            continue
        stream = streams[s]
        order, name = stream.order, stream.name
        axis = order[phase]
        n = SIZES[axis]
        d = 1 - 2 * di
        idx = list(me)
        for a in order[:phase]:
            idx[a] = slice(None)
        if phase:
            a = order[phase - 1]
            idx[a] = (me[a] + sub) % SIZES[a]
        idx[axis] = (me[axis] - d * (step - 1)) % n
        first, rows = stream.start, stream.rows
        if step == n // 2:
            cut = (rows // 32) * 16 if (s + phase) % 2 else -(-rows // 32) * 16
            first, rows = (first, cut) if di == 0 else (first + cut, rows - cut)
            if rows == 0:
                continue
        where = idx if len(order) == 3 else idx[2:]
        ref = outs[name].at[tuple(where) + (pl.ds(first, rows),)]
        src = ref
        if step == 1 and (phase == 0 or (phase == 1 and sub == 0)):
            src = sources[name].at[pl.ds(first, rows)]
        elif step == 1 and phase == 2:
            land(name)
        i = len(copies)
        c = pltpu.make_async_remote_copy(
            src, ref, send_sem.at[i], recv_sem.at[i],
            device_id={"ctx": neighbour(me, axis, d)}, device_id_type=MESH,
        )
        c.start()
        copies[key] = c
    for name in sources:
        land(name)
    for c in copies.values():
        c.wait_send()


def core(pay, val, exit_keys):
    z_only = (2,)
    streams = [Stream("pay", z_only, 0, 2 * HD)] + streams_of("val", V_UNITS)
    streams += [Stream("pay", z_only, 2 * HD, HD)]
    late = range(len(streams), len(streams) + 3)
    streams += streams_of("blk", K_UNITS)
    tasks = [(("chain", k), 0.45) for k in range(NZ - 1, -1, -1)] + [(("emit",), 0.6)]
    actions = plan(streams, late, (0,), tasks, [])
    n = sum(a[0] == "send" for a in actions)
    sd = jax.ShapeDtypeStruct
    return pl.pallas_call(
        functools.partial(core_kernel, streams, actions),
        name="core",
        out_shape=(
            sd((NZ,) + pay.shape, BF16),
            sd(SIZES + val.shape, BF16),
            sd(SIZES + (BLOCK, HD), BF16),
            sd((NZ - 1, 2 * HD, HD), BF16),
            sd((HD, HD), F32),
        ),
        in_specs=[VMEM] * 3,
        out_specs=(VMEM, ANY, ANY, VMEM, VMEM),
        scratch_shapes=[
            pltpu.VMEM((BLOCK, HD), BF16),
            pltpu.VMEM((HD, HD), F32),
            pltpu.VMEM((2, HD, HD), BF16),
            pltpu.VMEM((HD, HD), F32),
            pltpu.VMEM((HD, HD), F32),
            pltpu.SemaphoreType.DMA((n,)),
            pltpu.SemaphoreType.DMA((n,)),
            pltpu.SemaphoreType.DMA((3,)),
        ],
        compiler_params=pltpu.CompilerParams(collective_id=1, has_side_effects=True),
    )(pay, val, exit_keys)


V_UNITS, K_UNITS = (3, 3, 2), (4, 3, 3)


def streams_of(name, units):
    out, start = [], 0
    for order, u in zip(ORDERS, units):
        out.append(Stream(name, order, start * 16, u * 16))
        start += u
    return out


STEP = 4
TILE = 256


def attend_kernel(
    mask, gathered, values, group, inner, lead, mq, own, val, wo_hbm,
    mine_o, send_o,
    chosen, kv, slices, moves, run, keys, peak, total, acc, att, wo, part, kv_sem, misc_sem,
):
    position = lax.axis_index("ctx")
    me_group, head = position // NZ, lax.axis_index("head")
    w_load = pltpu.make_async_copy(wo_hbm, wo, misc_sem.at[0])
    g_load = pltpu.make_async_copy(gathered.at[:, :, SEG:BLOCK, :], slices, misc_sem.at[1])
    g_load.start()

    def scan(j, count):
        hit = mask[0, j] > 0

        @pl.when(hit)
        def _():
            chosen[count] = j

        return count + hit.astype(jnp.int32)

    count = jnp.minimum(lax.fori_loop(0, position, scan, jnp.int32(0)), MOST)
    chunks = (count + STEP - 1) // STEP

    def fetch(s, _):
        j = chosen[s]
        g, z = j // NZ, j % NZ

        pltpu.make_async_copy(values.at[g, z], kv.at[s, SEG : 2 * SEG], kv_sem.at[s]).start()

        @pl.when(g == me_group)
        def _():
            pltpu.make_async_copy(group.at[z, 2 * HD : 3 * HD], kv.at[s, 0:SEG], kv_sem.at[s]).start()

        @pl.when(g != me_group)
        def _():
            pltpu.make_async_copy(gathered.at[g, z, 0:SEG], kv.at[s, 0:SEG], kv_sem.at[s]).start()

        return 0

    lax.fori_loop(0, count, fetch, 0)
    w_load.start()

    def blank(s, _):
        kv[s] = jnp.zeros((2 * SEG, HD), BF16)
        return 0

    lax.fori_loop(count, chunks * STEP, blank, 0)

    v_own = val[...]
    for t in range(GROUP * SEG // TILE):
        sl = pl.ds(t * TILE, TILE)
        s = own[sl, :]
        top = jnp.broadcast_to(jnp.max(s, axis=1, keepdims=True), (TILE, HD))
        p = jnp.exp2(s - top)
        peak[sl, :] = top
        total[sl, :] = p
        acc[sl, :] = mm(p.astype(BF16), v_own)

    g_load.wait()

    run[...] = lead[...]

    def step_back(i, _):
        n = me_group - 1 - i
        r = run[...]
        store_pair(moves, n, r * SCALE2)
        g = (slices[n, :, 0:SLICE, :].reshape(HD, HD), slices[n, :, SLICE : 2 * SLICE, :].reshape(HD, HD))
        run[...] = dot3(g, r)
        return 0

    lax.fori_loop(0, me_group, step_back, 0)
    moves[NG : NG + NZ - 1] = inner[...]

    def chunk(c, _):
        for u in range(STEP):
            s = c * STEP + u

            @pl.when(s < count)
            def _():
                pltpu.make_async_copy(kv.at[s], kv.at[s], kv_sem.at[s]).wait()

        for u in range(STEP):
            s = c * STEP + u
            j = jnp.where(s < count, chosen[s], 0)
            which = jnp.where(j // NZ == me_group, NG + j % NZ, j // NZ)
            k = kv[s, 0:SEG, :]
            moved = mm(jnp.concatenate([k, k], axis=1), moves[which])
            keys[u * SEG : (u + 1) * SEG, :] = moved.astype(BF16)

        bias = jnp.concatenate(
            [jnp.full((1, SEG), jnp.where(c * STEP + u < count, 0.0, NEGATIVE), F32) for u in range(STEP)], axis=1
        )
        k_now = keys[...]
        v_now = jnp.concatenate([kv[c * STEP + u, SEG : 2 * SEG, :] for u in range(STEP)], axis=0)
        for t in range(GROUP * SEG // TILE):
            sl = pl.ds(t * TILE, TILE)
            s = mm(mq[sl, :], k_now, NT) + bias
            parts = [s[:, u * SEG : (u + 1) * SEG] for u in range(STEP)]
            high = parts[0]
            for x in parts[1:]:
                high = jnp.maximum(high, x)
            old = peak[sl, :]
            top = jnp.maximum(old, jnp.max(high, axis=1, keepdims=True))
            fade = jnp.exp2(old - top)
            ps = [jnp.exp2(x - top) for x in parts]
            peak[sl, :] = top
            total[sl, :] = total[sl, :] * fade + ((ps[0] + ps[1]) + (ps[2] + ps[3]))
            p = jnp.concatenate([x.astype(BF16) for x in ps], axis=1)
            acc[sl, :] = acc[sl, :] * fade + mm(p, v_now)
        return 0

    lax.fori_loop(0, chunks, chunk, 0)
    for g in range(GROUP):
        sl = pl.ds(g * SEG, SEG)
        out = acc[sl, :] / jnp.sum(total[sl, :], axis=1, keepdims=True)
        att[:, g * HD : (g + 1) * HD] = out.astype(BF16)
    w_load.wait()
    width = wo.shape[1]
    for c in range(0, width, 512):
        part[:, c : c + 512] = mm(att[...], wo[:, c : c + 512])
    half = SEG // 2
    mine_o[...] = part[pl.ds(pl.multiple_of(head * half, half), half), :]
    send_o[...] = part[pl.ds(pl.multiple_of((1 - head) * half, half), half), :].astype(BF16)


def attend(mask, gathered, values, group, inner, lead, mq, own, val, w_out):
    sd = jax.ShapeDtypeStruct
    width = w_out.shape[1]
    rows = GROUP * SEG
    return pl.pallas_call(
        attend_kernel,
        name="attend",
        out_shape=(sd((SEG // 2, width), F32), sd((SEG // 2, width), BF16)),
        in_specs=[SMEM, ANY, ANY, ANY, VMEM, VMEM, VMEM, VMEM, VMEM, ANY],
        out_specs=(VMEM, VMEM),
        scratch_shapes=[
            pltpu.SMEM((MOST,), jnp.int32),
            pltpu.VMEM((MOST, 2 * SEG, HD), BF16),
            pltpu.VMEM((NG, NZ, 2 * SLICE, HD), BF16),
            pltpu.VMEM((NG + NZ - 1, 2 * HD, HD), BF16),
            pltpu.VMEM((HD, HD), F32),
            pltpu.VMEM((STEP * SEG, HD), BF16),
            pltpu.VMEM((rows, HD), F32),
            pltpu.VMEM((rows, HD), F32),
            pltpu.VMEM((rows, HD), F32),
            pltpu.VMEM((SEG, GROUP * HD), BF16),
            pltpu.VMEM(w_out.shape, BF16),
            pltpu.VMEM((SEG, width), F32),
            pltpu.SemaphoreType.DMA((MOST,)),
            pltpu.SemaphoreType.DMA((2,)),
        ],
    )(mask, gathered.reshape(NG, NZ, BLOCK, HD), values.reshape(NG, NZ, SEG, HD), group, inner, lead, mq, own, val, w_out)


def body(
    hidden, w_query, w_key, w_value, w_dir, u_rate, rate_bias, q_gain, k_gain, w_out, block_mask
):
    theirs = swap(hidden, 0)
    mq, own, pay, exit_keys, val = segment(
        hidden, theirs, w_query, w_key, w_value, w_dir, u_rate, rate_bias, q_gain, k_gain
    )
    group, v_all, k_all, inner, lead = core(pay, val, exit_keys)
    mine, give = attend(block_mask, k_all, v_all, group, inner, lead, mq, own, val, w_out)
    got = swap(give, 3)
    return (mine + got.astype(F32)).astype(BF16)


def solution(mesh):
    in_specs = (
        P(("ctx", "head"), None),
        P(None, "head"),
        P(None, "head"),
        P(None, "head"),
        P(None, "head"),
        P("head", None),
        P("head"),
        P(),
        P(),
        P("head", None),
        P("ctx", None),
    )
    out_specs = P(("ctx", "head"), None)
    return jax.shard_map(body, mesh=mesh, in_specs=in_specs, out_specs=out_specs, check_vma=False)
```

```python
import functools
import heapq
import math

import jax
import jax.numpy as jnp
from jax import lax
from jax.experimental import pallas as pl
from jax.experimental.pallas import tpu as pltpu
from jax.sharding import PartitionSpec as P

HD = 128
SEG = 128
GROUP = 8
MOST = 32
SIZES = (4, 4, 8)
NX, NY, NZ = SIZES
NG = NX * NY
SLICE = SEG // NZ
BLOCK = SEG + 2 * SLICE
ORDERS = ((2, 1, 0), (0, 2, 1), (1, 0, 2))
EPSILON = 1e-06
NEGATIVE = -1e30
SCALE2 = math.log2(math.e) / math.sqrt(HD)
MESH = pl.DeviceIdType.MESH
F32, BF16 = jnp.float32, jnp.bfloat16
VMEM = pl.BlockSpec(memory_space=pltpu.VMEM)
SMEM = pl.BlockSpec(memory_space=pltpu.SMEM)
ANY = pl.BlockSpec(memory_space=pl.ANY)

NN = ((1,), (0,))
NT = ((1,), (1,))


def mm(a, b, dims=NN):
    return lax.dot_general(a, b, (dims, ((), ())), preferred_element_type=F32)


def split(x):
    hi = x.astype(BF16)
    return hi, (x - hi.astype(F32)).astype(BF16)


def dot3(a, b, dims=NN):
    ah, al = a if isinstance(a, tuple) else split(a)
    bh, bl = b if isinstance(b, tuple) else split(b)
    return mm(ah, bh, dims) + (mm(ah, bl, dims) + mm(al, bh, dims))


def coords():
    c = lax.axis_index("ctx")
    return c // (NY * NZ), (c // NZ) % NY, c % NZ


def neighbour(me, axis, delta):
    t = list(me)
    t[axis] = (me[axis] + delta) % SIZES[axis]
    return (t[0] * NY + t[1]) * NZ + t[2]


def swap_kernel(src, dst, send_sem, recv_sem):
    other = 1 - lax.axis_index("head")
    barrier = pltpu.get_barrier_semaphore()
    pl.semaphore_signal(barrier, inc=1, device_id={"head": other}, device_id_type=MESH)
    pl.semaphore_wait(barrier, 1)
    copy = pltpu.make_async_remote_copy(
        src, dst, send_sem, recv_sem, device_id={"head": other}, device_id_type=MESH
    )
    copy.start()
    copy.wait()


def swap(x, collective_id):
    return pl.pallas_call(
        swap_kernel,
        name="swap%d" % collective_id,
        out_shape=jax.ShapeDtypeStruct(x.shape, x.dtype),
        in_specs=[VMEM],
        out_specs=VMEM,
        scratch_shapes=[pltpu.SemaphoreType.DMA, pltpu.SemaphoreType.DMA],
        compiler_params=pltpu.CompilerParams(collective_id=collective_id, has_side_effects=True),
    )(x)


def segment_kernel(
    mine, theirs, wk, wv, wd, ur, rb, kg,
    pay_o, exit_o, val_o, both_o, solved_o, rows,
):
    head = lax.axis_index("head")
    half = SEG // 2
    rows[pl.ds(pl.multiple_of(head * half, half), half), :] = mine[...]
    rows[pl.ds(pl.multiple_of((1 - head) * half, half), half), :] = theirs[...]
    x = rows[...]
    ii = lax.broadcasted_iota(jnp.int32, (SEG, SEG), 0)
    jj = lax.broadcasted_iota(jnp.int32, (SEG, SEG), 1)
    strict = ii > jj
    eye = jnp.where(ii == jj, 1.0, 0.0).astype(F32)

    raw = mm(x, wd[...])
    dirs = raw * lax.rsqrt(jnp.sum(raw * raw, axis=1, keepdims=True) + EPSILON)
    key = mm(x, wk[...])
    key = key * lax.rsqrt(jnp.mean(key * key, axis=1, keepdims=True) + EPSILON) * kg[...]
    logit = jnp.sum(x.astype(F32) * ur[...].astype(F32), axis=1, keepdims=True) + rb[0]
    rate = 2.0 * jax.nn.sigmoid(logit)
    val_o[...] = mm(x, wv[...]).astype(BF16)

    both = jnp.concatenate([dirs, key], axis=0)
    both_s = split(both)
    dirs_s = (both_s[0][:SEG], both_s[1][:SEG])
    grams = dot3(dirs_s, both_s, NT)
    lower = jnp.where(strict, rate * grams[:, :SEG], 0.0)
    crossing = jnp.where(strict, grams[:, SEG:], 0.0)
    size = 1
    inverse = None
    while size < SEG:
        pick = (ii // (2 * size) == jj // (2 * size)) & (ii // size > jj // size)
        corner = jnp.where(pick, lower, 0.0)
        if inverse is None:
            inverse = eye - corner
        else:
            inv_s = split(inverse)
            inverse = inverse - dot3(dot3(inv_s, corner), inv_s)
        size *= 2
    solved = dot3(inverse, jnp.concatenate([rate * dirs, rate * crossing], axis=1))
    solved_s = split(solved)
    turned = dot3(split(solved.T), dirs_s)
    product_t = eye - turned[:SEG]
    exit_keys = key - turned[SEG:]
    hi, lo = split(product_t)
    pay_o[0:HD, :] = hi
    pay_o[HD : 2 * HD, :] = lo
    pay_o[2 * HD : 3 * HD, :] = exit_keys.astype(BF16)
    exit_o[...] = exit_keys

    both_o[0], both_o[1] = both_s
    solved_o[0], solved_o[1] = solved_s


def segment(mine, theirs, w_key, w_value, w_dir, u_rate, rate_bias, k_gain):
    sd = jax.ShapeDtypeStruct
    return pl.pallas_call(
        segment_kernel,
        name="segment",
        out_shape=(
            sd((3 * HD, SEG), BF16),
            sd((SEG, HD), F32),
            sd((SEG, HD), BF16),
            sd((2, 2 * SEG, HD), BF16),
            sd((2, SEG, 2 * HD), BF16),
            sd((SEG, w_key.shape[0]), BF16),
        ),
        in_specs=[VMEM, VMEM, VMEM, VMEM, VMEM, VMEM, SMEM, VMEM],
        out_specs=(VMEM,) * 6,
    )(mine, theirs, w_key, w_value, w_dir, u_rate, rate_bias, k_gain.reshape(1, HD))


def store_pair(ref, index, x):
    hi, lo = split(x)
    ref[index, 0:HD, :] = hi
    ref[index, HD : 2 * HD, :] = lo


LATENCY, WIRE = 3.0, 42e3


class Stream:
    def __init__(self, name, order, start, rows, direct=False, delay=0.0):
        self.name, self.order, self.start, self.rows = name, order, start, rows
        self.direct, self.delay = direct, delay


def plan(streams, late, needs, tasks, fillers):
    link, heap, actions, got = {}, [], [], {}
    clock = 0.0
    fillers, tasks = list(fillers), list(tasks)
    missing = sum(SIZES[streams[s].order[0]] - 1 for s in needs)

    def push(t, event):
        heapq.heappush(heap, (t, len(actions), event))

    def ring(s, phase, sub, pieces):
        far = SIZES[streams[s].order[phase]] // 2 if phase == 0 and streams[s].direct else 1
        for step in range(far, 0, -1):
            for di in (0, 1):
                send(s, phase, sub, step, di, pieces)

    def send(s, phase, sub, step, di, pieces):
        axis = streams[s].order[phase]
        share = 0.5 if step == SIZES[axis] // 2 else 1.0
        hops = step if phase == 0 and streams[s].direct else 1
        begin = max(link.get((axis, di), 0.0), clock)
        wire = streams[s].rows * HD * 2 * pieces * share / WIRE
        link[axis, di] = begin + wire * hops
        push(begin + wire + LATENCY + 0.75 * (hops - 1), ("wait", s, phase, sub, step, di, pieces))
        actions.append(("send", s, phase, sub, step, di))

    def launch(some):
        for s in some:
            for phase in range(min(2, len(streams[s].order))):
                ring(s, phase, 0, 1)

    launch(s for s in range(len(streams)) if s not in late and not streams[s].delay)
    for s in range(len(streams)):
        if s not in late and streams[s].delay:
            push(streams[s].delay, ("launch", s))
    while heap:
        t, _, event = heapq.heappop(heap)
        while fillers and t - clock > 0.6 * fillers[0][1]:
            actions.append(fillers[0][0])
            clock += fillers.pop(0)[1]
        clock = max(clock, t) + 0.03
        if event[0] == "launch":
            launch([event[1]])
            continue
        if event[0] == "task":
            name, cost = tasks.pop(0)
            actions.append(name)
            clock += cost
            if tasks:
                push(clock, ("task",))
            else:
                launch(late)
            continue
        _, s, phase, sub, step, di, pieces = event
        actions.append(("wait", s, phase, sub, step, di))
        order = streams[s].order
        n = SIZES[order[phase]]
        last = step == n // 2
        if not last and not (phase == 0 and streams[s].direct):
            send(s, phase, sub, step + 1, di, pieces)
        offset = step if di or last else -step
        got[s, phase, sub, offset] = got.get((s, phase, sub, offset), 0) + (1 if last else 2)
        if got[s, phase, sub, offset] < 2:
            continue
        if s in needs:
            missing -= 1
            if missing == 0:
                push(clock, ("task",))
        if len(order) == 1 or phase == 2:
            continue
        if phase == 0:
            ring(s, 1, offset, 1)
            done = (s, 0)
        else:
            done = (s, offset)
        got[done] = got.get(done, 0) + 1
        if phase == 0 and got[done] == n - 1:
            ring(s, 2, 0, n)
        elif phase == 1 and got[done] == SIZES[order[0]]:
            ring(s, 2, offset, SIZES[order[0]])
    return actions + [f[0] for f in fillers]


def greet(me, axes):
    barrier = pltpu.get_barrier_semaphore()
    count = 0
    for axis in axes:
        for d in range(1, SIZES[axis]):
            pl.semaphore_signal(
                barrier, inc=1, device_id={"ctx": neighbour(me, axis, d)}, device_id_type=MESH
            )
            count += 1
    pl.semaphore_wait(barrier, count)


def core_kernel(
    streams, actions,
    pay, val, exit_keys, both, solved, x, wq_hbm, qg,
    group, v_all, k_all, inner_o, lead_o, mq_o, own_o,
    blk, reach, whole, after, lead, wq, send_sem, recv_sem, own_sem,
):
    load = pltpu.make_async_copy(wq_hbm, wq, own_sem.at[3])
    load.start()
    me = coords()
    z = me[2]
    sources = {"pay": pay, "val": val, "blk": blk}
    outs = {"pay": group, "val": v_all, "blk": k_all}
    own = {
        name: pltpu.make_async_copy(
            sources[name], outs[name].at[(z,) if name == "pay" else tuple(me)], own_sem.at[i]
        )
        for i, name in enumerate(sources)
    }
    own["pay"].start()
    own["val"].start()
    greet(me, range(3))
    landed, copies = set(), {}

    def land(name):
        if name not in landed:
            own[name].wait()
            landed.add(name)

    def chain(k):
        if k == NZ - 1:
            land("pay")
            ii = lax.broadcasted_iota(jnp.int32, (HD, HD), 0)
            jj = lax.broadcasted_iota(jnp.int32, (HD, HD), 1)
            eye = jnp.where(ii == jj, 1.0, 0.0).astype(F32)
            reach[...] = eye
            lead[...] = eye
            after[...] = group[k, 0:HD, :].astype(F32) + group[k, HD : 2 * HD, :].astype(F32)
            return
        step = (group[k, 0:HD, :], group[k, HD : 2 * HD, :])

        @pl.when(z == k)
        def _():
            reach[...] = after[...]

        before = lead[...]
        store_pair(inner_o, k, before * SCALE2)
        lead[...] = jnp.where(k < z, dot3(step, before), before)
        after[...] = dot3(step, after[...])

    def emit():
        lead_o[...] = lead[...]
        hi, lo = split(after[...])
        whole[0] = hi
        whole[1] = lo
        part = pl.ds(pl.multiple_of(z * SLICE, SLICE), SLICE)
        blk[SEG : SEG + SLICE, :] = whole[0, part, :]
        blk[SEG + SLICE : BLOCK, :] = whole[1, part, :]
        blk[0:SEG, :] = dot3(exit_keys[...], reach[...]).astype(BF16)
        own["blk"].start()

    def head(g):
        if g == 0:
            load.wait()
        reach_mask = lax.broadcasted_iota(jnp.int32, (SEG, SEG), 0) >= lax.broadcasted_iota(jnp.int32, (SEG, SEG), 1)
        q2 = mm(x[...], wq[:, g * HD : (g + 2) * HD])
        for sub in range(2):
            q = q2[:, sub * HD : (sub + 1) * HD]
            q = q * lax.rsqrt(jnp.mean(q * q, axis=1, keepdims=True) + EPSILON) * qg[...]
            r = dot3(q, (both[0], both[1]), NT)
            near = jnp.where(reach_mask, r[:, :SEG], 0.0)
            moved = dot3(near, (solved[0], solved[1]))
            sl = slice((g + sub) * SEG, (g + sub + 1) * SEG)
            mq_o[sl, :] = (q - moved[:, :HD]).astype(BF16)
            own_o[sl, :] = jnp.where(reach_mask, (r[:, SEG:] - moved[:, HD:]) * SCALE2, NEGATIVE)

    for act in actions:
        if act[0] == "head":
            head(act[1])
            continue
        if act[0] == "chain":
            chain(act[1])
            continue
        if act[0] == "emit":
            emit()
            continue
        key = act[1:]
        s, phase, sub, step, di = key
        if act[0] == "wait":
            if key in copies:
                copies[key].wait_recv()
            continue
        stream = streams[s]
        order, name = stream.order, stream.name
        axis = order[phase]
        n = SIZES[axis]
        d = 1 - 2 * di
        far = phase == 0 and stream.direct
        idx = list(me)
        for a in order[:phase]:
            idx[a] = slice(None)
        if phase:
            a = order[phase - 1]
            idx[a] = (me[a] + sub) % SIZES[a]
        if not far:
            idx[axis] = (me[axis] - d * (step - 1)) % n
        first, rows = stream.start, stream.rows
        if step == n // 2:
            cut = (rows // 32) * 16 if (s + phase) % 2 else -(-rows // 32) * 16
            first, rows = (first, cut) if di == 0 else (first + cut, rows - cut)
            if rows == 0:
                continue
        where = idx if len(order) == 3 else idx[2:]
        ref = outs[name].at[tuple(where) + (pl.ds(first, rows),)]
        src = ref
        if far or (step == 1 and (phase == 0 or (phase == 1 and sub == 0))):
            src = sources[name].at[pl.ds(first, rows)]
        elif step == 1 and phase == 2:
            land(name)
        i = len(copies)
        c = pltpu.make_async_remote_copy(
            src, ref, send_sem.at[i], recv_sem.at[i],
            device_id={"ctx": neighbour(me, axis, d * step if far else d)}, device_id_type=MESH,
        )
        c.start()
        copies[key] = c
    for name in sources:
        land(name)
    for c in copies.values():
        c.wait_send()


def core(pay, val, exit_keys, both, solved, x, w_query, q_gain):
    z_only = (2,)
    streams = [Stream("pay", z_only, i * HD, HD, P_DIRECT) for i in range(2)]
    streams += streams_of("val", V_UNITS, V_DIRECT, V_DELAY)
    streams += [Stream("pay", z_only, 2 * HD, HD, False, V_DELAY)]
    first_late = len(streams)
    streams += streams_of("blk", K_UNITS, K_DIRECT)
    late = range(first_late, len(streams))
    tasks = [(("chain", k), 0.45) for k in range(NZ - 1, -1, -1)] + [(("emit",), 0.6)]
    fillers = [(("head", g), 0.9) for g in range(0, GROUP, 2)]
    actions = plan(streams, late, (0, 1), tasks, fillers)
    n = sum(a[0] == "send" for a in actions)
    sd = jax.ShapeDtypeStruct
    return pl.pallas_call(
        functools.partial(core_kernel, streams, actions),
        name="core",
        out_shape=(
            sd((NZ,) + pay.shape, BF16),
            sd(SIZES + val.shape, BF16),
            sd(SIZES + (BLOCK, HD), BF16),
            sd((NZ - 1, 2 * HD, HD), BF16),
            sd((HD, HD), F32),
            sd((GROUP * SEG, HD), BF16),
            sd((GROUP * SEG, SEG), F32),
        ),
        in_specs=[VMEM] * 6 + [ANY, VMEM],
        out_specs=(VMEM, ANY, ANY, VMEM, VMEM, VMEM, VMEM),
        scratch_shapes=[
            pltpu.VMEM((BLOCK, HD), BF16),
            pltpu.VMEM((HD, HD), F32),
            pltpu.VMEM((2, HD, HD), BF16),
            pltpu.VMEM((HD, HD), F32),
            pltpu.VMEM((HD, HD), F32),
            pltpu.VMEM(w_query.shape, BF16),
            pltpu.SemaphoreType.DMA((n,)),
            pltpu.SemaphoreType.DMA((n,)),
            pltpu.SemaphoreType.DMA((4,)),
        ],
        compiler_params=pltpu.CompilerParams(collective_id=1, has_side_effects=True),
    )(pay, val, exit_keys, both, solved, x, w_query, q_gain.reshape(1, HD))


V_UNITS, K_UNITS = (3, 3, 2), (4, 3, 3)
P_DIRECT, V_DIRECT, K_DIRECT, V_DELAY = False, True, True, 0.01


def streams_of(name, units, direct, delay=0.0):
    out, start = [], 0
    for order, u in zip(ORDERS, units):
        out.append(Stream(name, order, start * 16, u * 16, direct, delay))
        start += u
    return [x for x in out if x.rows]


STEP = 4
TILE = 256


def attend_kernel(
    mask, gathered, values, group, inner, lead, mq, own, val, wo_hbm,
    mine_o, send_o,
    chosen, kv, slices, moves, run, keys, peak, total, acc, att, wo, part, kv_sem, misc_sem,
):
    position = lax.axis_index("ctx")
    me_group, head = position // NZ, lax.axis_index("head")
    w_load = pltpu.make_async_copy(wo_hbm, wo, misc_sem.at[0])
    g_load = pltpu.make_async_copy(gathered.at[:, :, SEG:BLOCK, :], slices, misc_sem.at[1])
    g_load.start()

    def scan(j, count):
        hit = mask[0, j] > 0

        @pl.when(hit)
        def _():
            chosen[count] = j

        return count + hit.astype(jnp.int32)

    count = jnp.minimum(lax.fori_loop(0, position, scan, jnp.int32(0)), MOST)
    chunks = (count + STEP - 1) // STEP

    def fetch(s, _):
        j = chosen[s]
        g, z = j // NZ, j % NZ

        pltpu.make_async_copy(values.at[g, z], kv.at[s, SEG : 2 * SEG], kv_sem.at[s]).start()

        @pl.when(g == me_group)
        def _():
            pltpu.make_async_copy(group.at[z, 2 * HD : 3 * HD], kv.at[s, 0:SEG], kv_sem.at[s]).start()

        @pl.when(g != me_group)
        def _():
            pltpu.make_async_copy(gathered.at[g, z, 0:SEG], kv.at[s, 0:SEG], kv_sem.at[s]).start()

        return 0

    lax.fori_loop(0, count, fetch, 0)
    w_load.start()

    def blank(s, _):
        kv[s] = jnp.zeros((2 * SEG, HD), BF16)
        return 0

    lax.fori_loop(count, chunks * STEP, blank, 0)

    v_own = val[...]
    for t in range(GROUP * SEG // TILE):
        sl = pl.ds(t * TILE, TILE)
        s = own[sl, :]
        top = jnp.broadcast_to(jnp.max(s, axis=1, keepdims=True), (TILE, HD))
        p = jnp.exp2(s - top)
        peak[sl, :] = top
        total[sl, :] = p
        acc[sl, :] = mm(p.astype(BF16), v_own)

    g_load.wait()

    run[...] = lead[...]

    def step_back(i, _):
        n = me_group - 1 - i
        r = run[...]
        store_pair(moves, n, r * SCALE2)
        g = (slices[n, :, 0:SLICE, :].reshape(HD, HD), slices[n, :, SLICE : 2 * SLICE, :].reshape(HD, HD))
        run[...] = dot3(g, r)
        return 0

    lax.fori_loop(0, me_group, step_back, 0)
    moves[NG : NG + NZ - 1] = inner[...]

    def chunk(c, full):
        for u in range(STEP):
            s = c * STEP + u

            @pl.when(s < count)
            def _():
                pltpu.make_async_copy(kv.at[s], kv.at[s], kv_sem.at[s]).wait()

        for u in range(STEP):
            s = c * STEP + u
            j = chosen[s] if full else jnp.where(s < count, chosen[s], 0)
            which = jnp.where(j // NZ == me_group, NG + j % NZ, j // NZ)
            k = kv[s, 0:SEG, :]
            moved = mm(jnp.concatenate([k, k], axis=1), moves[which])
            keys[u * SEG : (u + 1) * SEG, :] = moved.astype(BF16)

        k_now = keys[...]
        v_now = jnp.concatenate([kv[c * STEP + u, SEG : 2 * SEG, :] for u in range(STEP)], axis=0)
        for t in range(GROUP * SEG // TILE):
            sl = pl.ds(t * TILE, TILE)
            s = mm(mq[sl, :], k_now, NT)
            parts = [s[:, u * SEG : (u + 1) * SEG] for u in range(STEP)]
            if not full:
                parts = [x + jnp.where(c * STEP + u < count, 0.0, NEGATIVE) for u, x in enumerate(parts)]
            high = functools.reduce(jnp.maximum, parts)
            old = peak[sl, :]
            top = jnp.maximum(old, jnp.max(high, axis=1, keepdims=True))
            fade = jnp.exp2(old - top)
            ps = [jnp.exp2(x - top) for x in parts]
            peak[sl, :] = top
            total[sl, :] = total[sl, :] * fade + functools.reduce(jnp.add, ps)
            p = jnp.concatenate([x.astype(BF16) for x in ps], axis=1)
            acc[sl, :] = acc[sl, :] * fade + mm(p, v_now)

    whole_chunks = count // STEP

    def full_chunk(c, _):
        chunk(c, True)
        return 0

    lax.fori_loop(0, whole_chunks, full_chunk, 0)

    @pl.when(whole_chunks < chunks)
    def _():
        chunk(whole_chunks, False)

    for g in range(GROUP):
        sl = pl.ds(g * SEG, SEG)
        out = acc[sl, :] / jnp.sum(total[sl, :], axis=1, keepdims=True)
        att[:, g * HD : (g + 1) * HD] = out.astype(BF16)
    w_load.wait()
    width = wo.shape[1]
    for c in range(0, width, 512):
        part[:, c : c + 512] = mm(att[...], wo[:, c : c + 512])
    half = SEG // 2
    mine_o[...] = part[pl.ds(pl.multiple_of(head * half, half), half), :]
    send_o[...] = part[pl.ds(pl.multiple_of((1 - head) * half, half), half), :].astype(BF16)


def attend(mask, gathered, values, group, inner, lead, mq, own, val, w_out):
    sd = jax.ShapeDtypeStruct
    width = w_out.shape[1]
    rows = GROUP * SEG
    return pl.pallas_call(
        attend_kernel,
        name="attend",
        out_shape=(sd((SEG // 2, width), F32), sd((SEG // 2, width), BF16)),
        in_specs=[SMEM, ANY, ANY, ANY, VMEM, VMEM, VMEM, VMEM, VMEM, ANY],
        out_specs=(VMEM, VMEM),
        scratch_shapes=[
            pltpu.SMEM((MOST,), jnp.int32),
            pltpu.VMEM((MOST, 2 * SEG, HD), BF16),
            pltpu.VMEM((NG, NZ, 2 * SLICE, HD), BF16),
            pltpu.VMEM((NG + NZ - 1, 2 * HD, HD), BF16),
            pltpu.VMEM((HD, HD), F32),
            pltpu.VMEM((STEP * SEG, HD), BF16),
            pltpu.VMEM((rows, HD), F32),
            pltpu.VMEM((rows, HD), F32),
            pltpu.VMEM((rows, HD), F32),
            pltpu.VMEM((SEG, GROUP * HD), BF16),
            pltpu.VMEM(w_out.shape, BF16),
            pltpu.VMEM((SEG, width), F32),
            pltpu.SemaphoreType.DMA((MOST,)),
            pltpu.SemaphoreType.DMA((2,)),
        ],
    )(mask, gathered.reshape(NG, NZ, BLOCK, HD), values.reshape(NG, NZ, SEG, HD), group, inner, lead, mq, own, val, w_out)


def body(
    hidden, w_query, w_key, w_value, w_dir, u_rate, rate_bias, q_gain, k_gain, w_out, block_mask
):
    theirs = swap(hidden, 0)
    pay, exit_keys, val, both, solved, rows = segment(
        hidden, theirs, w_key, w_value, w_dir, u_rate, rate_bias, k_gain
    )
    group, v_all, k_all, inner, lead, mq, own = core(
        pay, val, exit_keys, both, solved, rows, w_query, q_gain
    )
    mine, give = attend(block_mask, k_all, v_all, group, inner, lead, mq, own, val, w_out)
    got = swap(give, 3)
    return (mine + got.astype(F32)).astype(BF16)


def solution(mesh):
    in_specs = (
        P(("ctx", "head"), None),
        P(None, "head"),
        P(None, "head"),
        P(None, "head"),
        P(None, "head"),
        P("head", None),
        P("head"),
        P(),
        P(),
        P("head", None),
        P("ctx", None),
    )
    out_specs = P(("ctx", "head"), None)
    return jax.shard_map(body, mesh=mesh, in_specs=in_specs, out_specs=out_specs, check_vma=False)
```
